32 devices in a mesh: gy: 8 (over y, x, core), gx: 4 (over z).
Axes of the slice: x: 2, y: 2, z: 4, core: 2. Of those that a mesh axis runs over, the one named last changes fastest.
Arguments:
- feat_a: float32 [512, 256, 128], P('gy', 'gx'), may hold values from -8 to 8
- feat_b: float32 [512, 256, 128], P('gy', 'gx'), may hold values from -8 to 8
- occ_a: int32 [512, 256], P('gy', 'gx'), may hold values from 0 to 1, as said below
- occ_b: int32 [512, 256], P('gy', 'gx'), may hold values from 0 to 1, as said below
- first_weight: bfloat16 [256, 256], replicated, may hold values from -0.375 to 0.375
- second_weight: bfloat16 [256, 128], replicated, may hold values from -0.375 to 0.375
Outputs:
- matched_a: float32 [512, 256, 128], P('gy', 'gx')
- matched_b: float32 [512, 256, 128], P('gy', 'gx')
The draws below stay inside these ranges and needn't reach their ends.
Inputs may be any that keep to these rules, and one draw needn't show every extreme that they name: `occ_a`: 1 marks an occupied cell. `occ_b`: 1 marks an occupied cell.
All inputs are finite; a program needn't handle non-finite values.
Results may differ from the reference program's by a relative error of at most 0.0042.
Values may be sent and summed in bfloat16 or wider, within the bound.
A program may use at most 64 MiB of HBM per device.

```python
import jax
import jax.numpy as jnp
from jax import lax

C = 128
H = 256
R = 8
NY = 512
NX = 256


def feature_pair(key):
    keys_list = jax.random.split(jax.random.fold_in(key, 7101), 5)
    first = jax.random.normal(keys_list[3], (NY, NX, C), jnp.float32)
    second = jax.random.normal(keys_list[4], (NY, NX, C), jnp.float32)
    return (jnp.clip(first, -8.0, 8.0), jnp.clip(second, -8.0, 8.0))


def draw_feat_a(key, part):
    return feature_pair(key)[0]


def draw_feat_b(key, part):
    return feature_pair(key)[1]


def occupied_cells(key):
    keys_list = jax.random.split(key, 3)
    patch_level = jax.random.randint(keys_list[0], (NY // 8 + 1, NX // 32 + 1), 0, 4)
    region_level = jax.random.randint(keys_list[1], (NY // 64 + 1, NX // 256 + 1), 1, 4)
    row_iota = jnp.arange(NY, dtype=jnp.int32)
    col_iota = jnp.arange(NX, dtype=jnp.int32)
    patches = patch_level[row_iota // 8][:, col_iota // 32]
    regions = region_level[row_iota // 64][:, col_iota // 256]
    threshold = patches * regions * 11
    rolled = jax.random.randint(keys_list[2], (NY, NX), 0, 100)
    return (rolled < threshold).astype(jnp.int32)


def draw_occ_a(key, part):
    return occupied_cells(jax.random.fold_in(key, 5201))


def draw_occ_b(key, part):
    return occupied_cells(jax.random.fold_in(key, 5202))


def normal_values(key, extent, deviation, reach, held_as=jnp.bfloat16):
    return jnp.clip(deviation * jax.random.normal(key, extent, jnp.float32), -reach, reach).astype(held_as)


def setup_inputs(seed: int = 0) -> dict:
    key_of = jax.random.split(jax.random.key(seed), 7)
    feat_a = draw_feat_a(jax.random.fold_in(key_of[6], 71), 0)
    feat_b = draw_feat_b(jax.random.fold_in(key_of[6], 71), 0)
    occ_a = draw_occ_a(jax.random.fold_in(key_of[6], 71), 0)
    occ_b = draw_occ_b(jax.random.fold_in(key_of[6], 71), 0)
    first_weight = normal_values(key_of[4], (2 * C, H), (2 * C) ** -0.5, 0.375)
    second_weight = normal_values(key_of[5], (H, C), H ** -0.5, 0.375)
    return dict(feat_a=feat_a, feat_b=feat_b, occ_a=occ_a, occ_b=occ_b, first_weight=first_weight, second_weight=second_weight)


def transport(queries, keys, key_mask):
    window = 2 * R + 1
    scaling = 1.0 / (C ** 0.5)
    query_full = queries.astype(jnp.float32)
    key_padded = jnp.pad(keys.astype(jnp.float32), ((R, R), (R, R), (0, 0)))
    mask_padded = jnp.pad(key_mask.astype(jnp.float32), ((R, R), (R, R)))
    offsets = jnp.arange(window * window, dtype=jnp.int32)

    def one_band(band_index):
        top_row = band_index * 8
        query_band = lax.dynamic_slice(query_full, (top_row, jnp.int32(0), jnp.int32(0)), (8, NX, C))

        def key_at(offset):
            down_step = offset // window
            across = offset % window
            key_band = lax.dynamic_slice(key_padded, (top_row + down_step, across, jnp.int32(0)), (8, NX, C))
            mask_band = lax.dynamic_slice(mask_padded, (top_row + down_step, across), (8, NX))
            return key_band, mask_band

        def score_at(offset):
            key_band, mask_band = key_at(offset)
            return jnp.sum(query_band * key_band, axis=-1) * scaling, mask_band

        cost_stack, mask_stack = lax.map(score_at, offsets)
        usable = mask_stack > 0
        highest = jnp.max(jnp.where(usable, cost_stack, 0.0), axis=0)
        exponent = jnp.where(usable, jnp.exp(cost_stack - highest), 0.0)
        denominator = jnp.exp(-highest) + jnp.sum(exponent, axis=0)
        weights = lax.optimization_barrier((exponent / denominator).astype(jnp.bfloat16)).astype(jnp.float32)

        def accumulate(carried, element):
            offset, weight = element
            key_band, unused = key_at(offset)
            return carried + weight[..., None] * key_band, None

        gathered, unused = lax.scan(accumulate, jnp.zeros((8, NX, C), jnp.float32), (offsets, weights))
        return gathered

    band_list = lax.map(one_band, jnp.arange(NY // 8, dtype=jnp.int32))
    return band_list.reshape(NY, NX, C)


def refine(feature, half, carried, cell_mask, first_weight, second_weight):
    joined = jnp.concatenate([half, carried.astype(jnp.bfloat16)], axis=-1).reshape(-1, 2 * C)
    hidden = jax.nn.gelu(jnp.dot(joined, first_weight, preferred_element_type=jnp.float32), approximate=False).astype(jnp.bfloat16)
    update = jnp.dot(hidden, second_weight, preferred_element_type=jnp.float32).reshape(feature.shape)
    return feature + cell_mask.astype(jnp.float32)[..., None] * update


def reference(feat_a, feat_b, occ_a, occ_b, first_weight, second_weight):
    for repeat in range(2):
        half_a = feat_a.astype(jnp.bfloat16)
        half_b = feat_b.astype(jnp.bfloat16)
        carried_a = transport(half_a, half_b, occ_b)
        carried_b = transport(half_b, half_a, occ_a)
        feat_a = refine(feat_a, half_a, carried_a, occ_a, first_weight, second_weight)
        feat_b = refine(feat_b, half_b, carried_b, occ_b, first_weight, second_weight)
    return feat_a, feat_b
```

```python
import functools

import jax
import jax.numpy as jnp
import numpy as np
from jax import lax
from jax.experimental import pallas as pl
from jax.experimental.pallas import tpu as pltpu
from jax.sharding import PartitionSpec as P

R = 8
band = 8
tile_width = 16
key_rows = band + 2 * R
key_width = tile_width + 2 * R
BLOCKED = -1e30
OCC_LANE = band + tile_width
ONE_LANE = OCC_LANE + 1


def extended(cells, sides, width):
    for axis, dim in sides:
        count = lax.axis_size(axis)
        ends = count - 1
        head = lax.slice_in_dim(cells, 0, width, axis=dim)
        tail = lax.slice_in_dim(cells, cells.shape[dim] - width, cells.shape[dim], axis=dim)
        cells = jnp.concatenate(
            [
                lax.ppermute(tail, axis, [(i, (i + 1) % count) for i in range(ends)]),
                cells,
                lax.ppermute(head, axis, [((i + 1) % count, i) for i in range(ends)]),
            ],
            axis=dim,
        )
    return cells


def band_lanes(channels):
    keys = np.zeros((key_rows, key_width, channels), np.float32)
    down = np.arange(key_rows)
    side = np.arange(key_width)
    for i in range(band):
        keys[(down < i) | (down > i + 2 * R), :, i] = BLOCKED
    for i in range(tile_width):
        keys[:, (side < i) | (side > i + 2 * R), band + i] = BLOCKED
    keys[:, :, ONE_LANE] = 1.0
    queries = np.zeros((band, tile_width, channels), np.float32)
    for i in range(band):
        queries[i, :, i] = 1.0
    for i in range(tile_width):
        queries[:, i, band + i] = 1.0
    queries[:, :, OCC_LANE] = 1.0
    return (
        jnp.asarray(queries.reshape(-1, channels), jnp.bfloat16),
        jnp.asarray(keys.reshape(-1, channels), jnp.bfloat16),
    )


def gelu(x):
    size = jnp.abs(x)
    t = 1.0 / (1.0 + (0.3275911 * 0.5**0.5) * size)
    series = 0.5 * 1.061405429
    for a in (-1.453152027, 1.421413741, -0.284496736, 0.254829592):
        series = series * t + 0.5 * a
    tail = series * t * jnp.exp2((-0.5 / np.log(2.0)) * (x * x))
    return jnp.maximum(x, 0.0) - size * tail


def one_tile(feat, keys, bias, cell_mask, query_lanes, first, second):
    channels = feat.shape[-1]
    rate = 1.0 / (channels**0.5 * np.log(2.0))
    half = feat.astype(jnp.bfloat16)
    queries = jnp.concatenate([half, query_lanes], axis=1)
    wide = jnp.concatenate([keys, bias], axis=1)
    scores = lax.dot_general(
        queries, wide, (((1,), (1,)), ((), ())), preferred_element_type=jnp.float32
    )
    highest = jnp.maximum(jnp.max(scores, axis=1, keepdims=True), 0.0)
    exponent = jnp.exp2((scores - highest) * rate).astype(jnp.bfloat16)
    total = jnp.dot(exponent, wide, preferred_element_type=jnp.float32)
    denominator = jnp.exp2(-highest * rate) + total[:, channels + ONE_LANE : channels + ONE_LANE + 1]
    carried = (total[:, :channels] * (1.0 / denominator)).astype(jnp.bfloat16)
    joined = jnp.concatenate([half, carried], axis=1)
    hidden = gelu(jnp.dot(joined, first, preferred_element_type=jnp.float32)).astype(jnp.bfloat16)
    update = jnp.dot(hidden, second, preferred_element_type=jnp.float32)
    return feat + cell_mask.astype(jnp.float32) * update


def pass_kernel(
    feat_a, feat_b, mask_a, mask_b, keys_a, keys_b, bias_a, bias_b, query_lanes, key_lanes,
    first, second, *outs,
):
    top = pl.multiple_of(pl.program_id(0) * band, band)
    channels = feat_a.shape[-1]

    def cells(ref, left):
        return ref[:, pl.ds(left, tile_width), :].reshape(-1, channels)

    def window(ref, left):
        return ref[pl.ds(top, key_rows), pl.ds(left, key_width), :].reshape(-1, channels)

    def step(tile, carry):
        left = pl.multiple_of(tile * tile_width, tile_width)
        for i, (feat, keys, bias, mask) in enumerate(
            ((feat_a, keys_b, bias_b, mask_a), (feat_b, keys_a, bias_a, mask_b))
        ):
            new = one_tile(
                cells(feat, left),
                window(keys, left),
                window(bias, left) + key_lanes[...],
                cells(mask, left),
                query_lanes[...],
                first[...],
                second[...],
            ).reshape(band, tile_width, channels)
            outs[i][:, pl.ds(left, tile_width), :] = new
            if len(outs) > 2:
                outs[i + 2][:, pl.ds(left, tile_width), :] = new.astype(jnp.bfloat16)
        return carry

    lax.fori_loop(0, feat_a.shape[1] // tile_width, step, 0)


def one_pass(feats, masks, keys, biases, weights, halves):
    rows, cols, channels = feats[0].shape
    query_lanes, key_lanes = band_lanes(channels)
    strip = pl.BlockSpec((band, cols, channels), lambda i: (i, 0, 0))

    def whole(x):
        return pl.BlockSpec(x.shape, lambda i: (0,) * x.ndim)

    rest = (*keys, *biases, query_lanes, key_lanes, *weights)
    out_shape = [jax.ShapeDtypeStruct(feats[0].shape, jnp.float32)] * 2
    if halves:
        out_shape += [jax.ShapeDtypeStruct(feats[0].shape, jnp.bfloat16)] * 2
    return pl.pallas_call(
        pass_kernel,
        grid=(rows // band,),
        in_specs=[strip] * 4 + [whole(x) for x in rest],
        out_specs=[strip] * len(out_shape),
        out_shape=out_shape,
        compiler_params=pltpu.CompilerParams(vmem_limit_bytes=56 * 2**20),
    )(*feats, *masks, *rest)


def halo(half_a, half_b):
    both = extended(jnp.stack([half_a, half_b]), (("gy", 1), ("gx", 2)), R)
    return both[0], both[1]


def spread(mask, lane_values):
    return (mask[..., None] * lane_values).astype(jnp.bfloat16)


def local(feat_a, feat_b, occ_a, occ_b, first_weight, second_weight):
    channels = feat_a.shape[-1]
    weights = (first_weight, second_weight)
    feats = (feat_a, feat_b)
    ones = jnp.ones((channels,), jnp.bfloat16)
    masks = tuple(spread(occ.astype(jnp.bfloat16), ones) for occ in (occ_a, occ_b))
    occs = halo(occ_a.astype(jnp.bfloat16), occ_b.astype(jnp.bfloat16))
    lane = jnp.where(jnp.arange(channels) == OCC_LANE, BLOCKED, 0.0).astype(jnp.bfloat16)
    biases = tuple(spread(1 - occ, lane) for occ in occs)
    keys = halo(feat_a.astype(jnp.bfloat16), feat_b.astype(jnp.bfloat16))
    new_a, new_b, half_a, half_b = one_pass(feats, masks, keys, biases, weights, True)
    keys = halo(half_a, half_b)
    return tuple(one_pass((new_a, new_b), masks, keys, biases, weights, False))


def solution(mesh):
    in_specs = (P("gy", "gx", None), P("gy", "gx", None), P("gy", "gx"), P("gy", "gx"), P(), P())
    out_specs = (P("gy", "gx", None), P("gy", "gx", None))
    return jax.shard_map(local, mesh=mesh, in_specs=in_specs, out_specs=out_specs, check_vma=False)
```

```python
import functools

import jax
import jax.numpy as jnp
import numpy as np
from jax import lax
from jax.experimental import pallas as pl
from jax.experimental.pallas import tpu as pltpu
from jax.sharding import PartitionSpec as P

R = 8
band = 8
tile_width = 16
key_rows = band + 2 * R
key_width = tile_width + 2 * R
chunk = band * key_width
BLOCKED = -1e30
COL_LANE = 3 * band
EMPTY_LANE = COL_LANE + 2 * tile_width
ONE_LANE = EMPTY_LANE + 1
EMPTY = 2.0**20


def halo_kernel(half_a, half_b, ext_a, ext_b, send_sems, recv_sems, *, axes):
    rows, cols, channels = half_a.shape
    me = [lax.axis_index(axis) for axis in axes]
    counts = [lax.axis_size(axis) for axis in axes]
    ways = [(dy, dx) for dy in (-1, 0, 1) for dx in (-1, 0, 1) if (dy, dx) != (0, 0)]

    def present(way):
        there = [m + d for m, d in zip(me, way)]
        ok = None
        for t, d, n in zip(there, way, counts):
            if d:
                test = (t >= 0) if d < 0 else (t < n)
                ok = test if ok is None else jnp.logical_and(ok, test)
        return ok

    def edge(d, size):
        return {-1: (0, R), 0: (0, size), 1: (size - R, R)}[d]

    def landing(d, size):
        return {-1: (R + size, R), 0: (R, size), 1: (0, R)}[d]

    def copy(i, way, survey):
        y, x = edge(way[0], rows), edge(way[1], cols)
        to_y, to_x = landing(way[0], rows), landing(way[1], cols)
        half, ext = ((half_a, ext_a), (half_b, ext_b))[survey]
        return pltpu.make_async_remote_copy(
            src_ref=half.at[pl.ds(*y), pl.ds(*x)],
            dst_ref=ext.at[pl.ds(*to_y), pl.ds(*to_x)],
            send_sem=send_sems.at[survey, i],
            recv_sem=recv_sems.at[survey, i],
            device_id=(me[0] + way[0], me[1] + way[1]),
            device_id_type=pl.DeviceIdType.MESH,
        )

    barrier = pltpu.get_barrier_semaphore()
    for way in ways:

        @pl.when(present(way))
        def _(way=way):
            pl.semaphore_signal(
                barrier,
                inc=1,
                device_id=(me[0] + way[0], me[1] + way[1]),
                device_id_type=pl.DeviceIdType.MESH,
            )

    near = [jnp.where(m > 0, 2, 1) + jnp.where(m < n - 1, 1, 0) for m, n in zip(me, counts)]
    pl.semaphore_wait(barrier, near[0] * near[1] - 1)

    for i, way in enumerate(ways):

        @pl.when(present(way))
        def _(i=i, way=way):
            copy(i, way, 0).start()
            copy(i, way, 1).start()

    def move(row, carry):
        for half, ext in ((half_a, ext_a), (half_b, ext_b)):
            ext[R + row, pl.ds(R, cols), :] = half[row]
        return carry

    lax.fori_loop(0, rows, move, 0)

    for i, way in enumerate(ways):
        source = (-way[0], -way[1])

        @pl.when(present(way))
        def _(i=i, way=way):
            copy(i, way, 0).wait_send()
            copy(i, way, 1).wait_send()

        @pl.when(present(source))
        def _(i=i, way=way):
            copy(i, way, 0).wait_recv()
            copy(i, way, 1).wait_recv()

        @pl.when(jnp.logical_not(present(source)))
        def _(way=way):
            (y, height), (x, width) = landing(way[0], rows), landing(way[1], cols)

            def fill(row, carry):
                for ext in (ext_a, ext_b):
                    ext[row, pl.ds(x, width), :] = jnp.full((width, channels), EMPTY, ext.dtype)
                return carry

            lax.fori_loop(y, y + height, fill, 0)


def halo(half_a, half_b, index):
    rows, cols, channels = half_a.shape
    ext = jax.ShapeDtypeStruct((rows + 2 * R, cols + 2 * R, channels), half_a.dtype)
    return pl.pallas_call(
        functools.partial(halo_kernel, axes=("gy", "gx")),
        out_shape=[ext] * 2,
        in_specs=[pl.BlockSpec(memory_space=pltpu.VMEM)] * 2,
        out_specs=[pl.BlockSpec(memory_space=pltpu.VMEM)] * 2,
        scratch_shapes=[pltpu.SemaphoreType.DMA((2, 8)), pltpu.SemaphoreType.DMA((2, 8))],
        compiler_params=pltpu.CompilerParams(collective_id=index, has_side_effects=True),
    )(half_a, half_b)


def query_kinds(channels):
    lanes = np.zeros((3, 2, band, tile_width, channels), np.float32)
    for kind in range(3):
        for i in range(band):
            lanes[kind, :, i, :, kind * band + i] = 1.0
    for kind in range(2):
        for i in range(tile_width):
            lanes[:, kind, :, i, COL_LANE + kind * tile_width + i] = 1.0
    lanes[..., EMPTY_LANE] = 1.0
    return jnp.asarray(lanes.reshape(6, band * tile_width, channels), jnp.bfloat16)


def key_pattern(cols, channels):
    y = np.arange(3 * band)[:, None, None]
    x = np.arange(cols)[None, :, None]
    lane = np.arange(channels)[None, None, :]
    part = (y // band - lane // band) % 3
    row, want_row = y % band, lane % band
    row_out = (lane < COL_LANE) & (((part == 0) & (row < want_row)) | ((part == 2) & (row > want_row)))
    col_lane = lane - COL_LANE
    first = (x // tile_width) % 2 == col_lane // tile_width
    col, want_col = x % tile_width, col_lane % tile_width
    col_out = (
        (lane >= COL_LANE)
        & (lane < EMPTY_LANE)
        & ((first & (col < want_col)) | (~first & (col > want_col)))
    )
    one = np.where(lane == ONE_LANE, 1.0, 0.0)
    return jnp.asarray(np.where(row_out | col_out, BLOCKED, one), jnp.bfloat16)


def gelu(x):
    return x * (0.5 * lax.erf(x * 0.5**0.5) + 0.5)


def pass_kernel(
    feat_a, feat_b, keys_a, keys_b, pattern, kinds, first, second, *refs, halves
):
    outs = refs[: 4 if halves else 2]
    lanes_a, lanes_b, scores_a, scores_b, peak_a, peak_b, joined_a, joined_b = refs[len(outs) :]
    strip, cols, channels = feat_a.shape
    across = cols // tile_width
    count = (strip // band) * across
    rate = 1.0 / (channels**0.5 * np.log(2.0))
    feats, keys, lanes = (feat_a, feat_b), (keys_b, keys_a), (lanes_b, lanes_a)
    own = (keys_a, keys_b)
    scores, peaks, joins = (scores_a, scores_b), (peak_a, peak_b), (joined_a, joined_b)
    step_index = pl.program_id(0)

    @pl.when(step_index == 0)
    def _():
        lane = lax.broadcasted_iota(jnp.int32, (keys_a.shape[1], channels), 1)
        empty = jnp.where(lane == EMPTY_LANE, BLOCKED, 0.0).astype(jnp.bfloat16)
        zero = jnp.zeros_like(empty)

        def fill(row, carry):
            base = pattern[row % (3 * band)]
            for key, lane_ref in ((keys_a, lanes_a), (keys_b, lanes_b)):
                lane_ref[row] = base + jnp.where(key[row] >= EMPTY, empty, zero)
            return carry

        lax.fori_loop(0, keys_a.shape[0], fill, 0)

    def place(tile):
        tile = jnp.clip(tile, 0, count - 1)
        down, side = tile // across, tile % across
        inside = pl.multiple_of(down * band, band)
        top = pl.multiple_of(step_index * strip + inside, band)
        return inside, top, pl.multiple_of(side * tile_width, tile_width)

    def cells(s, tile):
        inside, _, left = place(tile)
        return feats[s][pl.ds(inside, band), pl.ds(left, tile_width), :].reshape(-1, channels)

    def wide(s, tile, part):
        _, top, left = place(tile)
        at = (pl.ds(pl.multiple_of(top + part * band, band), band), pl.ds(left, key_width))
        return jnp.concatenate(
            [keys[s][at].reshape(-1, channels), lanes[s][at].reshape(-1, channels)], axis=1
        )

    def half_step(s_new, tile_new, s_old, tile_old, s_mlp, tile_mlp):
        _, top, left = place(tile_new)
        kind = ((top // band) % 3) * 2 + (left // tile_width) % 2
        queries = jnp.concatenate([cells(s_new, tile_new).astype(jnp.bfloat16), kinds[kind]], axis=1)
        old_peak = peaks[s_old][...]
        old_top = jnp.concatenate([old_peak, old_peak], axis=1)
        best = None
        total = None
        hidden_in = jnp.dot(joins[s_mlp][...], first[...], preferred_element_type=jnp.float32)
        for part in range(3):
            got = lax.dot_general(
                queries,
                wide(s_new, tile_new, part),
                (((1,), (1,)), ((), ())),
                preferred_element_type=jnp.float32,
            )
            weight = jnp.exp2((scores[s_old][part] - old_top) * rate).astype(jnp.bfloat16)
            term = jnp.dot(weight, wide(s_old, tile_old, part), preferred_element_type=jnp.float32)
            total = term if part == 0 else total + term
            scores[s_new][part] = got
            high = jnp.maximum(got[:, :channels], got[:, channels:])
            best = high if part == 0 else jnp.maximum(best, high)
            if part == 0:
                hidden = gelu(hidden_in).astype(jnp.bfloat16)
            if part == 1:
                update = jnp.dot(hidden, second[...], preferred_element_type=jnp.float32)
        peaks[s_new][...] = jnp.broadcast_to(
            jnp.maximum(jnp.max(best, axis=1, keepdims=True), 0.0), best.shape
        )
        mass = channels + ONE_LANE
        denominator = jnp.exp2(-old_peak * rate) + total[:, mass : mass + 1]
        carried = total[:, :channels] / denominator
        inside, top, left = place(tile_mlp)
        held = own[s_mlp][pl.ds(pl.multiple_of(top + R, R), band), pl.ds(pl.multiple_of(left + R, R), tile_width), :]
        held = held.reshape(-1, channels).astype(jnp.float32) < EMPTY
        new = cells(s_mlp, tile_mlp) + jnp.where(held, update, 0.0)
        sent = jnp.where(held, new, EMPTY).reshape(band, tile_width, channels)
        new = new.reshape(band, tile_width, channels)
        at = (pl.ds(inside, band), pl.ds(left, tile_width))
        outs[s_mlp][at] = new
        if halves:
            outs[s_mlp + 2][at] = sent.astype(jnp.bfloat16)
        joins[s_old][:, :channels] = cells(s_old, tile_old).astype(jnp.bfloat16)
        joins[s_old][:, channels:] = carried.astype(jnp.bfloat16)

    def step(tile, carry):
        half_step(0, tile, 1, tile - 1, 0, tile - 1)
        half_step(1, tile, 0, tile, 1, tile - 1)
        return carry

    lax.fori_loop(0, count + 1, step, 0)


def one_pass(feats, keys, weights, halves):
    rows, cols, channels = feats[0].shape
    height = 2 * band if rows % (2 * band) == 0 else band
    strip = pl.BlockSpec((height, cols, channels), lambda i: (i, 0, 0))
    cells = band * tile_width

    def whole(x):
        return pl.BlockSpec(x.shape, lambda i: (0,) * x.ndim)

    rest = (*keys, key_pattern(keys[0].shape[1], channels), query_kinds(channels), *weights)
    out_shape = [jax.ShapeDtypeStruct(feats[0].shape, jnp.float32)] * 2
    if halves:
        out_shape += [jax.ShapeDtypeStruct(feats[0].shape, jnp.bfloat16)] * 2
    return pl.pallas_call(
        functools.partial(pass_kernel, halves=halves),
        grid=(rows // height,),
        in_specs=[strip] * 2 + [whole(x) for x in rest],
        out_specs=[strip] * len(out_shape),
        out_shape=out_shape,
        scratch_shapes=[pltpu.VMEM(keys[0].shape, jnp.bfloat16)] * 2
        + [pltpu.VMEM((3, cells, chunk), jnp.float32)] * 2
        + [pltpu.VMEM((cells, channels), jnp.float32)] * 2
        + [pltpu.VMEM((cells, 2 * channels), jnp.bfloat16)] * 2,
        compiler_params=pltpu.CompilerParams(vmem_limit_bytes=56 * 2**20),
    )(*feats, *rest)


def keyed(feat, occ):
    return jnp.where(occ[..., None] > 0, feat, EMPTY).astype(jnp.bfloat16)


def local(feat_a, feat_b, occ_a, occ_b, first_weight, second_weight):
    weights = (first_weight, second_weight)
    keys = halo(keyed(feat_a, occ_a), keyed(feat_b, occ_b), 0)
    new_a, new_b, half_a, half_b = one_pass((feat_a, feat_b), keys, weights, True)
    keys = halo(half_a, half_b, 1)
    return tuple(one_pass((new_a, new_b), keys, weights, False))


def solution(mesh):
    in_specs = (P("gy", "gx", None), P("gy", "gx", None), P("gy", "gx"), P("gy", "gx"), P(), P())
    out_specs = (P("gy", "gx", None), P("gy", "gx", None))
    return jax.shard_map(local, mesh=mesh, in_specs=in_specs, out_specs=out_specs, check_vma=False)
```

```python
import functools

import jax
import jax.numpy as jnp
import numpy as np
from jax import lax
from jax.experimental import pallas as pl
from jax.experimental.pallas import tpu as pltpu
from jax.sharding import PartitionSpec as P

R = 8
band = 8
tile_width = 16
key_rows = band + 2 * R
key_width = tile_width + 2 * R
chunk = band * key_width
BLOCKED = -1e30
COL_LANE = 3 * band
EMPTY_LANE = COL_LANE + 2 * tile_width
ONE_LANE = EMPTY_LANE + 1
EMPTY = 2.0**20


def halo_kernel(half_a, half_b, ext_a, ext_b, send_sems, recv_sems, *, axes):
    rows, cols, channels = half_a.shape
    me = [lax.axis_index(axis) for axis in axes]
    counts = [lax.axis_size(axis) for axis in axes]
    ways = [(0, -1), (0, 1), (-1, -1), (-1, 1), (1, -1), (1, 1), (-1, 0), (1, 0)]

    def present(way):
        there = [m + d for m, d in zip(me, way)]
        ok = None
        for t, d, n in zip(there, way, counts):
            if d:
                test = (t >= 0) if d < 0 else (t < n)
                ok = test if ok is None else jnp.logical_and(ok, test)
        return ok

    def edge(d, size):
        return {-1: (0, R), 0: (0, size), 1: (size - R, R)}[d]

    def landing(d, size):
        return {-1: (R + size, R), 0: (R, size), 1: (0, R)}[d]

    def copy(i, way, survey):
        y, x = edge(way[0], rows), edge(way[1], cols)
        to_y, to_x = landing(way[0], rows), landing(way[1], cols)
        half, ext = ((half_a, ext_a), (half_b, ext_b))[survey]
        return pltpu.make_async_remote_copy(
            src_ref=half.at[pl.ds(*y), pl.ds(*x)],
            dst_ref=ext.at[pl.ds(*to_y), pl.ds(*to_x)],
            send_sem=send_sems.at[survey, i],
            recv_sem=recv_sems.at[survey, i],
            device_id=(me[0] + way[0], me[1] + way[1]),
            device_id_type=pl.DeviceIdType.MESH,
        )

    barrier = pltpu.get_barrier_semaphore()
    for way in ways:

        @pl.when(present(way))
        def _(way=way):
            pl.semaphore_signal(
                barrier,
                inc=1,
                device_id=(me[0] + way[0], me[1] + way[1]),
                device_id_type=pl.DeviceIdType.MESH,
            )

    near = [jnp.where(m > 0, 2, 1) + jnp.where(m < n - 1, 1, 0) for m, n in zip(me, counts)]
    pl.semaphore_wait(barrier, near[0] * near[1] - 1)

    for i, way in enumerate(ways):

        @pl.when(present(way))
        def _(i=i, way=way):
            copy(i, way, 0).start()
            copy(i, way, 1).start()

    def move(row, carry):
        for half, ext in ((half_a, ext_a), (half_b, ext_b)):
            ext[R + row, pl.ds(R, cols), :] = half[row]
        return carry

    lax.fori_loop(0, rows, move, 0, unroll=8)

    for way in ways:
        source = (-way[0], -way[1])

        @pl.when(jnp.logical_not(present(source)))
        def _(way=way):
            (y, height), (x, width) = landing(way[0], rows), landing(way[1], cols)

            def fill(row, carry):
                for ext in (ext_a, ext_b):
                    ext[row, pl.ds(x, width), :] = jnp.full((width, channels), EMPTY, ext.dtype)
                return carry

            lax.fori_loop(y, y + height, fill, 0)

    for i, way in enumerate(ways):
        source = (-way[0], -way[1])

        @pl.when(present(way))
        def _(i=i, way=way):
            copy(i, way, 0).wait_send()
            copy(i, way, 1).wait_send()

        @pl.when(present(source))
        def _(i=i, way=way):
            copy(i, way, 0).wait_recv()
            copy(i, way, 1).wait_recv()


def halo(half_a, half_b, index):
    rows, cols, channels = half_a.shape
    ext = jax.ShapeDtypeStruct((rows + 2 * R, cols + 2 * R, channels), half_a.dtype)
    return pl.pallas_call(
        functools.partial(halo_kernel, axes=("gy", "gx")),
        out_shape=[ext] * 2,
        in_specs=[pl.BlockSpec(memory_space=pltpu.VMEM)] * 2,
        out_specs=[pl.BlockSpec(memory_space=pltpu.VMEM)] * 2,
        scratch_shapes=[pltpu.SemaphoreType.DMA((2, 8)), pltpu.SemaphoreType.DMA((2, 8))],
        compiler_params=pltpu.CompilerParams(collective_id=index, has_side_effects=True),
    )(half_a, half_b)


def query_kinds(channels):
    lanes = np.zeros((3, 2, band, tile_width, channels), np.float32)
    for kind in range(3):
        for i in range(band):
            lanes[kind, :, i, :, kind * band + i] = 1.0
    for kind in range(2):
        for i in range(tile_width):
            lanes[:, kind, :, i, COL_LANE + kind * tile_width + i] = 1.0
    lanes[..., EMPTY_LANE] = 1.0
    return jnp.asarray(lanes.reshape(6, band * tile_width, channels), jnp.bfloat16)


def key_pattern(cols, channels):
    y = np.arange(3 * band)[:, None, None]
    x = np.arange(cols)[None, :, None]
    lane = np.arange(channels)[None, None, :]
    part = (y // band - lane // band) % 3
    row, want_row = y % band, lane % band
    row_out = (lane < COL_LANE) & (((part == 0) & (row < want_row)) | ((part == 2) & (row > want_row)))
    col_lane = lane - COL_LANE
    first = (x // tile_width) % 2 == col_lane // tile_width
    col, want_col = x % tile_width, col_lane % tile_width
    col_out = (
        (lane >= COL_LANE)
        & (lane < EMPTY_LANE)
        & ((first & (col < want_col)) | (~first & (col > want_col)))
    )
    one = np.where(lane == ONE_LANE, 1.0, 0.0)
    return jnp.asarray(np.where(row_out | col_out, BLOCKED, one), jnp.bfloat16)


def gelu(x):
    return x * (0.5 * lax.erf(x * 0.5**0.5) + 0.5)


def pass_kernel(
    feat_a, feat_b, keys_a, keys_b, pattern, kinds, first, second, *refs, halves
):
    outs = refs[: 4 if halves else 2]
    lanes_a, lanes_b, scores_a, scores_b, peak_a, peak_b, joined_a, joined_b = refs[len(outs) :]
    strip, cols, channels = feat_a.shape
    across = cols // tile_width
    count = (strip // band) * across
    rate = 1.0 / (channels**0.5 * np.log(2.0))
    feats, keys, lanes = (feat_a, feat_b), (keys_b, keys_a), (lanes_b, lanes_a)
    own = (keys_a, keys_b)
    scores, peaks, joins = (scores_a, scores_b), (peak_a, peak_b), (joined_a, joined_b)
    step_index = pl.program_id(0)

    @pl.when(step_index == 0)
    def _():
        lane = lax.broadcasted_iota(jnp.int32, (keys_a.shape[1], channels), 1)
        empty = jnp.where(lane == EMPTY_LANE, BLOCKED, 0.0).astype(jnp.bfloat16)
        zero = jnp.zeros_like(empty)

        def fill(row, carry):
            base = pattern[row % (3 * band)]
            for key, lane_ref in ((keys_a, lanes_a), (keys_b, lanes_b)):
                lane_ref[row] = base + jnp.where(key[row] >= EMPTY, empty, zero)
            return carry

        lax.fori_loop(0, keys_a.shape[0], fill, 0, unroll=8)

    def place(tile):
        tile = jnp.clip(tile, 0, count - 1)
        down, side = tile // across, tile % across
        inside = pl.multiple_of(down * band, band)
        top = pl.multiple_of(step_index * strip + inside, band)
        return inside, top, pl.multiple_of(side * tile_width, tile_width)

    def cells(s, tile):
        inside, _, left = place(tile)
        return feats[s][pl.ds(inside, band), pl.ds(left, tile_width), :].reshape(-1, channels)

    def wide(s, tile, part):
        _, top, left = place(tile)
        at = (pl.ds(pl.multiple_of(top + part * band, band), band), pl.ds(left, key_width))
        return jnp.concatenate(
            [keys[s][at].reshape(-1, channels), lanes[s][at].reshape(-1, channels)], axis=1
        )

    def half_step(s_new, tile_new, s_old, tile_old, s_mlp, tile_mlp):
        _, top, left = place(tile_new)
        kind = ((top // band) % 3) * 2 + (left // tile_width) % 2
        queries = jnp.concatenate([cells(s_new, tile_new).astype(jnp.bfloat16), kinds[kind]], axis=1)
        old_peak = peaks[s_old][...]
        old_top = jnp.concatenate([old_peak, old_peak], axis=1)
        best = None
        total = None
        hidden_in = jnp.dot(joins[s_mlp][...], first[...], preferred_element_type=jnp.float32)
        for part in range(3):
            got = lax.dot_general(
                queries,
                wide(s_new, tile_new, part),
                (((1,), (1,)), ((), ())),
                preferred_element_type=jnp.float32,
            )
            weight = jnp.exp2((scores[s_old][part] - old_top) * rate).astype(jnp.bfloat16)
            term = jnp.dot(weight, wide(s_old, tile_old, part), preferred_element_type=jnp.float32)
            total = term if part == 0 else total + term
            scores[s_new][part] = got
            high = jnp.maximum(got[:, :channels], got[:, channels:])
            best = high if part == 0 else jnp.maximum(best, high)
            if part == 0:
                hidden = gelu(hidden_in).astype(jnp.bfloat16)
            if part == 1:
                update = jnp.dot(hidden, second[...], preferred_element_type=jnp.float32)
        peaks[s_new][...] = jnp.broadcast_to(
            jnp.maximum(jnp.max(best, axis=1, keepdims=True), 0.0), best.shape
        )
        mass = channels + ONE_LANE
        denominator = jnp.exp2(-old_peak * rate) + total[:, mass : mass + 1]
        carried = total[:, :channels] / denominator
        inside, top, left = place(tile_mlp)
        held = own[s_mlp][pl.ds(pl.multiple_of(top + R, R), band), pl.ds(pl.multiple_of(left + R, R), tile_width), :]
        held = held.reshape(-1, channels).astype(jnp.float32) < EMPTY
        new = cells(s_mlp, tile_mlp) + jnp.where(held, update, 0.0)
        sent = jnp.where(held, new, EMPTY).reshape(band, tile_width, channels)
        new = new.reshape(band, tile_width, channels)
        at = (pl.ds(inside, band), pl.ds(left, tile_width))
        outs[s_mlp][at] = new
        if halves:
            outs[s_mlp + 2][at] = sent.astype(jnp.bfloat16)
        joins[s_old][:, :channels] = cells(s_old, tile_old).astype(jnp.bfloat16)
        joins[s_old][:, channels:] = carried.astype(jnp.bfloat16)

    def step(tile, carry):
        half_step(0, tile, 1, tile - 1, 0, tile - 1)
        half_step(1, tile, 0, tile, 1, tile - 1)
        return carry

    lax.fori_loop(0, count + 1, step, 0)


def one_pass(feats, keys, weights, halves):
    rows, cols, channels = feats[0].shape
    height = next(k * band for k in (4, 2, 1) if rows % (k * band) == 0)
    strip = pl.BlockSpec((height, cols, channels), lambda i: (i, 0, 0))
    cells = band * tile_width

    def whole(x):
        return pl.BlockSpec(x.shape, lambda i: (0,) * x.ndim)

    rest = (*keys, key_pattern(keys[0].shape[1], channels), query_kinds(channels), *weights)
    out_shape = [jax.ShapeDtypeStruct(feats[0].shape, jnp.float32)] * 2
    if halves:
        out_shape += [jax.ShapeDtypeStruct(feats[0].shape, jnp.bfloat16)] * 2
    return pl.pallas_call(
        functools.partial(pass_kernel, halves=halves),
        grid=(rows // height,),
        in_specs=[strip] * 2 + [whole(x) for x in rest],
        out_specs=[strip] * len(out_shape),
        out_shape=out_shape,
        scratch_shapes=[pltpu.VMEM(keys[0].shape, jnp.bfloat16)] * 2
        + [pltpu.VMEM((3, cells, chunk), jnp.float32)] * 2
        + [pltpu.VMEM((cells, channels), jnp.float32)] * 2
        + [pltpu.VMEM((cells, 2 * channels), jnp.bfloat16)] * 2,
        compiler_params=pltpu.CompilerParams(vmem_limit_bytes=56 * 2**20),
    )(*feats, *rest)


def keyed(feat, occ):
    return jnp.where(occ[..., None] > 0, feat, EMPTY).astype(jnp.bfloat16)


def local(feat_a, feat_b, occ_a, occ_b, first_weight, second_weight):
    weights = (first_weight, second_weight)
    keys = halo(keyed(feat_a, occ_a), keyed(feat_b, occ_b), 0)
    new_a, new_b, half_a, half_b = one_pass((feat_a, feat_b), keys, weights, True)
    keys = halo(half_a, half_b, 1)
    return tuple(one_pass((new_a, new_b), keys, weights, False))


def solution(mesh):
    in_specs = (P("gy", "gx", None), P("gy", "gx", None), P("gy", "gx"), P("gy", "gx"), P(), P())
    out_specs = (P("gy", "gx", None), P("gy", "gx", None))
    return jax.shard_map(local, mesh=mesh, in_specs=in_specs, out_specs=out_specs, check_vma=False)
```
